128 devices in a mesh: rep: 4 (over y), tp: 8 (over z, core), ep: 4 (over x).
Axes of the slice: x: 4, y: 4, z: 4, core: 2. Of those that a mesh axis runs over, the one named last changes fastest.
Arguments:
- prm_tokens: bfloat16 [8192, 4096], P(('rep', 'tp', 'ep')), may hold values from -6 to 6
- expert_ids: int32 [8192, 8], P(('rep', 'tp', 'ep')), may hold values from 0 to 63, all different within a row; in each aligned block of 64 rows (0 to 63, 64 to 127, ...) at most 10 rows name the same one
- combine_weights: float32 [8192, 8], P(('rep', 'tp', 'ep')), may hold values from 0.02 to 0.5
- w_gate: bfloat16 [64, 4096, 1536], P(('tp', 'ep'), None, 'rep'), may hold values from -0.09375 to 0.09375
- w_up: bfloat16 [64, 4096, 1536], P(('tp', 'ep'), None, 'rep'), may hold values from -0.09375 to 0.09375
- w_down: bfloat16 [64, 4096, 1536], P(('tp', 'ep'), None, 'rep'), may hold values from -0.15625 to 0.15625
Outputs:
- moe_out: bfloat16 [8192, 4096], P(('rep', 'tp', 'ep'))
The draws below stay inside these ranges and needn't reach their ends.
Inputs may be any that keep to these rules, and one draw needn't show every extreme that they name: `expert_ids`: within the rows of one device (aligned blocks of 64 rows) no expert is named by more than 10 rows, and some expert reaches 10 there.
All inputs are finite; a program needn't handle non-finite values.
Results may differ from the reference program's by a relative error of at most 0.012.
Values may be sent and summed in bfloat16 or wider, within the bound.
A program may use at most 192 MiB of HBM per device.

```python
import math
import jax
import jax.numpy as jnp
import numpy as np
from jax import lax

D = 4096
FFE = 1536
TOPK = 8
PT_DEV = 64
EXPERTS = 64
CAP = 10
PTOK = 8192
N_REP = 4
DEVICES = 128


def level_of(stream_key, extent, split, low, largest):
    level = 1.0
    for dim, shards_of in split:
        steps = jax.random.uniform(jax.random.fold_in(jax.random.fold_in(stream_key, 6), dim), (shards_of,), jnp.float32, low / len(split), largest / len(split))
        level = level * jnp.repeat(jnp.exp(steps), extent[dim] // shards_of).reshape((-1,) + (1,) * (len(extent) - 1 - dim))
    return level


def deal_out(stream_key, own, number, rows, number_of, top, limit, slope):
    ranking = jax.random.permutation(stream_key, number_of)
    crowded, usual = load_shares(number_of, rows * top, limit, slope, True), load_shares(number_of, rows * top, limit, slope, False)
    places = jnp.arange(number_of)

    def named(lengths, rotation):
        used = int((lengths > 0).sum())
        fixed = max(1, used // 4)
        passed = fixed + (places - fixed + rotation * (used - fixed)) % max(1, number_of - fixed)
        return jnp.zeros((number_of,), jnp.int32).at[ranking[jnp.where(places < fixed, places, passed)]].set(jnp.asarray(lengths, jnp.int32))

    lengths = jnp.where(number % 4 == 0, named(crowded, number // 4), named(usual, number - number // 4 - 1))
    mixed = jax.random.permutation(jax.random.fold_in(own, 3), number_of)
    giver, taker = mixed[0:number_of // 2 * 2:2], mixed[1:number_of // 2 * 2:2]
    margin = jnp.minimum(lengths[giver] - 1, limit - lengths[taker]) // 2
    margin = jnp.where((giver == ranking[0]) | (taker == ranking[0]) | (lengths[taker] == 0), 0, jnp.maximum(margin, 0))
    passed = jax.random.randint(jax.random.fold_in(own, 4), (number_of // 2,), 0, 1 << 20) % (margin + 1)
    lengths = lengths.at[giver].add(-passed).at[taker].add(passed)
    items = jnp.searchsorted(jnp.cumsum(lengths), jnp.arange(rows * top), side="right").astype(jnp.int32)
    grid = items.reshape(top, rows).T
    grid = grid[jax.random.permutation(jax.random.fold_in(own, 1), rows)]
    rotation = jax.random.randint(jax.random.fold_in(own, 2), (rows, 1), 0, top)
    return jnp.take_along_axis(grid, (jnp.arange(top)[None, :] + rotation) % top, axis=1)


def load_shares(number_of, total, limit, slope, full):
    weights = [(1 << 20) // math.isqrt(rank ** slope) + 1 for rank in range(1, number_of + 1)]
    largest = limit if full else min(limit, max(-(-total // number_of), total * weights[0] // sum(weights)))
    least = 1 if total - largest >= number_of - 1 else 0
    counts, spare = [largest] + [least] * (number_of - 1), total - largest - least * (number_of - 1)
    while spare > 0:
        movable = [i for i in range(1, number_of) if counts[i] < largest] or [i for i in range(1, number_of) if counts[i] < limit]
        whole, remaining = sum([weights[i] for i in movable]), spare
        for i in movable:
            more = min(limit - counts[i], max(1, remaining * weights[i] // whole), spare)
            counts[i] = counts[i] + more
            spare = spare - more
    return np.array(counts)


def normal_values(own_key, shape, scale, most, pieces=(), kind=jnp.bfloat16):
    entries = scale * jax.random.normal(own_key, shape, jnp.float32)
    if pieces:
        entries = entries * level_of(own_key, shape, pieces, -0.22, 0.18)
    return jnp.clip(entries, -most, most).astype(kind)


def setup_inputs(seed: int = 0) -> dict:
    key_of = jax.random.split(jax.random.key(seed), 7)
    prm_tokens = normal_values(key_of[0], (PTOK, D), 1.0, 6.0, ((0, 128),))
    expert_ids_keys = jax.random.split(jax.random.fold_in(key_of[1], 1), PTOK // PT_DEV)
    expert_ids_turns = jax.random.permutation(jax.random.fold_in(key_of[1], 3), PTOK // PT_DEV)
    expert_ids = jax.vmap(lambda own, number: deal_out(jax.random.fold_in(key_of[1], 2), own, number, PT_DEV, EXPERTS, TOPK, CAP, 2))(expert_ids_keys, expert_ids_turns).reshape((PTOK, TOPK))
    combine_weights = jnp.clip(jnp.exp(math.log(0.5) - 3.218876 * jax.random.uniform(key_of[2], (PTOK, TOPK), jnp.float32) ** level_of(key_of[2], (PTOK, TOPK), ((0, 128),), -0.2, 0.2)), 0.02, 0.5)
    w_gate = normal_values(key_of[3], (EXPERTS, D, FFE), D ** -0.5, 0.09375, ((0, 32), (2, 4)))
    w_up = normal_values(key_of[4], (EXPERTS, D, FFE), D ** -0.5, 0.09375, ((0, 32), (2, 4)))
    w_down = normal_values(key_of[5], (EXPERTS, D, FFE), FFE ** -0.5, 0.15625, ((0, 32), (2, 4)))
    return dict(prm_tokens=prm_tokens, expert_ids=expert_ids, combine_weights=combine_weights, w_gate=w_gate, w_up=w_up, w_down=w_down)


def expert_rows(token_rows, w_gate, w_up, w_down):
    gate_proj = jnp.dot(token_rows, w_gate, preferred_element_type=jnp.float32)
    upward = jnp.dot(token_rows, w_up, preferred_element_type=jnp.float32)
    hidden = (jax.nn.silu(gate_proj) * upward).astype(jnp.bfloat16)
    width = FFE // N_REP
    total = jnp.zeros((token_rows.shape[0], D), jnp.float32)
    for quarter in range(N_REP):
        part_hidden = hidden[:, quarter * width:(quarter + 1) * width]
        part_down = w_down[:, quarter * width:(quarter + 1) * width]
        piece = lax.dot_general(part_hidden, part_down, (((1,), (1,)), ((), ())), preferred_element_type=jnp.float32)
        total = total + piece.astype(jnp.bfloat16).astype(jnp.float32)
    return total.astype(jnp.bfloat16)


def reference(prm_tokens, expert_ids, combine_weights, w_gate, w_up, w_down):
    block_count = DEVICES
    block_ids = expert_ids.reshape(block_count, PT_DEV * TOPK)
    onehot = (block_ids[:, :, None] == jnp.arange(EXPERTS, dtype=jnp.int32)[None, None, :]).astype(jnp.int32)
    slot_rank = jnp.sum((jnp.cumsum(onehot, axis=1) - onehot) * onehot, axis=2)
    device_rows = jnp.arange(block_count, dtype=jnp.int32)[:, None]
    places = (block_ids * (block_count * CAP) + device_rows * CAP + slot_rank).reshape(-1).astype(jnp.int32)
    token_index = (jnp.arange(PTOK * TOPK, dtype=jnp.int32) // TOPK).astype(jnp.int32)
    source_table = jnp.full((EXPERTS * block_count * CAP,), PTOK, jnp.int32).at[places].set(token_index)
    padded = jnp.concatenate([prm_tokens, jnp.zeros((1, D), prm_tokens.dtype)], axis=0)
    buffers = padded[source_table].reshape(EXPERTS, block_count * CAP, D)

    def apply_expert(bundle):
        return expert_rows(bundle[0], bundle[1], bundle[2], bundle[3])

    outputs = lax.map(apply_expert, (buffers, w_gate, w_up, w_down))
    picked = outputs.reshape(-1, D)[places].astype(jnp.float32).reshape(PTOK, TOPK, D)
    moe_out = jnp.sum(picked * combine_weights[:, :, None], axis=1).astype(jnp.bfloat16)
    return moe_out
```

```python
import functools

import jax
import jax.numpy as jnp
from jax import lax
from jax.experimental import pallas as pl
from jax.experimental.pallas import tpu as pltpu
from jax.sharding import PartitionSpec as P

MESH = pl.DeviceIdType.MESH
BF = jnp.bfloat16
F32 = jnp.float32
TB = 64
D = 4096
W = 1408
HID = 384
CAP = 10
GROUPS = 16
ROWS = 512
SLOTS = 160


def places():
    y, tp, x = lax.axis_index("rep"), lax.axis_index("tp"), lax.axis_index("ep")

    def step(axis, by):
        if axis == "y":
            return (lax.rem(y + by + 4, 4), tp, x)
        if axis == "z":
            return (y, lax.rem(tp + 2 * by + 8, 8), x)
        return (y, tp, lax.rem(x + by + 4, 4))

    sibling = (y, tp + 1 - 2 * lax.rem(tp, 2), x)
    return step, sibling


def greet(step, sibling):
    barrier = pltpu.get_barrier_semaphore()
    for axis in "xyz":
        for by in (1, -1):
            pl.semaphore_signal(barrier, inc=1, device_id=step(axis, by), device_id_type=MESH)
    pl.semaphore_signal(barrier, inc=1, device_id=sibling, device_id_type=MESH)
    pl.semaphore_wait(barrier, 7)


ORDER = (("x", "y", "z"), ("y", "z", "x"), ("z", "x", "y"))
H2 = TB // 2


def gather_kernel(x_ref, o0, o1, o2, send_sem, recv_sem, loc_sem):
    step, sibling = places()
    outs = (o0, o1, o2)
    started = []

    def copy(k, idx, src, dst, dev):
        return pltpu.make_async_remote_copy(
            src_ref=src,
            dst_ref=dst,
            send_sem=send_sem.at[k, idx],
            recv_sem=recv_sem.at[k, idx],
            device_id=dev,
            device_id_type=MESH,
        )

    plan = []
    for k in range(3):
        a, b, c = ORDER[k]
        r = outs[k].at[0]
        own = x_ref.at[k]
        g = {}
        n = [0]

        def add(name, src, dst, dev):
            g[name] = copy(k, n[0], src, dst, dev)
            n[0] += 1

        add("a1", own, r.at[0, 0, 1], step(a, 1))
        add("a3", own, r.at[0, 0, 3], step(a, -1))
        add("a2l", r.at[0, 0, 1, pl.ds(0, H2)], r.at[0, 0, 2, pl.ds(0, H2)], step(a, 1))
        add("a2h", r.at[0, 0, 3, pl.ds(H2, H2)], r.at[0, 0, 2, pl.ds(H2, H2)], step(a, -1))
        for i in range(4):
            src = own if i == 0 else r.at[0, 0, i]
            add(f"b1{i}", src, r.at[0, 1, i], step(b, 1))
            add(f"b3{i}", src, r.at[0, 3, i], step(b, -1))
        for i in (0, 1):
            add(f"b2{i}", r.at[0, 1, i], r.at[0, 2, i], step(b, 1))
        for i in (2, 3):
            add(f"b2{i}", r.at[0, 3, i], r.at[0, 2, i], step(b, -1))
        for i in range(4):
            add(f"c1{i}", r.at[0, i], r.at[1, i], step(c, 1))
            add(f"c3{i}", r.at[0, i], r.at[3, i], step(c, -1))
            add(f"c2l{i}", r.at[1, i, pl.ds(0, 2)], r.at[2, i, pl.ds(0, 2)], step(c, 1))
            add(f"c2h{i}", r.at[3, i, pl.ds(2, 2)], r.at[2, i, pl.ds(2, 2)], step(c, -1))
        for j in range(4):
            for i in range(4):
                add(f"s{j}{i}", r.at[j, i], outs[k].at[1, j, i], sibling)
        plan.append(g)

    def go(k, *names):
        for name in names:
            plan[k][name].start()
            started.append(plan[k][name])

    def got(k, *names):
        for name in names:
            plan[k][name].wait_recv()

    local = [
        pltpu.make_async_copy(x_ref.at[k], outs[k].at[0, 0, 0, 0], loc_sem.at[k]) for k in range(3)
    ]
    for cp in local:
        cp.start()
    greet(step, sibling)
    for k in range(3):
        go(k, "a1", "a3")
    for k in range(3):
        go(k, "b10", "b30")
    for cp in local:
        cp.wait()
    for k in range(3):
        got(k, "a1")
        go(k, "a2l", "b11", "b31")
        got(k, "a3")
        go(k, "a2h", "b13", "b33")
    for k in range(3):
        got(k, "a2l", "a2h")
        go(k, "b12", "b32", "c10", "c30", "s00")
    for k in range(3):
        got(k, "b10")
        go(k, "b20")
        got(k, "b11")
        go(k, "b21")
        got(k, "b33")
        go(k, "b23")
    for k in range(3):
        got(k, "b32")
        go(k, "b22")
        got(k, "b12", "b13")
        go(k, "c11", "c31", "s01")
    for k in range(3):
        got(k, "b30", "b31")
        go(k, "c13", "c33", "s03")
    for k in range(3):
        got(k, "c10")
        go(k, "c2l0", "s10")
        got(k, "c30")
        go(k, "c2h0", "s30")
    for k in range(3):
        got(k, "b20", "b21", "b22", "b23")
        go(k, "c12", "c32", "s02")
    for i in (1, 3, 2):
        for k in range(3):
            got(k, f"c1{i}")
            go(k, f"c2l{i}", f"s1{i}")
            got(k, f"c3{i}")
            go(k, f"c2h{i}", f"s3{i}")
        j = {1: 0, 3: 1, 2: 3}[i]
        for k in range(3):
            got(k, f"c2l{j}", f"c2h{j}")
            go(k, f"s2{j}")
    for k in range(3):
        got(k, "c2l2", "c2h2")
        go(k, "s22")
    for k in range(3):
        for j in range(4):
            for i in range(4):
                got(k, f"s{j}{i}")
    for cp in started:
        cp.wait_send()


def gather_tokens(xs):
    shape = jax.ShapeDtypeStruct((2, 4, 4, 4, TB, W), BF)
    return pl.pallas_call(
        gather_kernel,
        out_shape=(shape,) * 3,
        in_specs=[pl.BlockSpec(memory_space=pltpu.VMEM)],
        out_specs=(pl.BlockSpec(memory_space=pl.ANY),) * 3,
        scratch_shapes=[
            pltpu.SemaphoreType.DMA((3, 48)),
            pltpu.SemaphoreType.DMA((3, 48)),
            pltpu.SemaphoreType.DMA((3,)),
        ],
        compiler_params=pltpu.CompilerParams(collective_id=1, has_side_effects=True),
        name="gather_tokens",
    )(xs)


def select_kernel(e_ref, x0, x1, x2, tri_ref, rows_ref, st_ref, w_ref):
    first = e_ref[0].astype(F32)
    xa = x0[...].reshape(ROWS, W)
    xb = jnp.concatenate([x1[0, :, 0, i].reshape(4 * TB, W) for i in range(2)], axis=0)
    xc = jnp.concatenate([x2[0, i, :, 0].reshape(4 * TB, W) for i in range(2)], axis=0)
    meta = xc[:, D - 2 * W :].astype(F32)
    lane = lax.broadcasted_iota(jnp.int32, (ROWS, 128), 1)
    member = jnp.zeros((ROWS, 128), F32)
    weight = jnp.zeros((ROWS, 128), F32)
    for e in range(2):
        hit = jnp.where((meta == first + e) & (lane < 8), 1.0, 0.0)
        moved = pltpu.roll(hit, 8, 1) + pltpu.roll(hit, 16, 1) + pltpu.roll(hit, 24, 1)
        named = jnp.sum(hit, axis=1, keepdims=True)
        value = jnp.sum(moved * meta, axis=1, keepdims=True)
        member = jnp.where(lane == e, named, member)
        weight = jnp.where(lane == e, value, weight)
    rank = jnp.dot(tri_ref[...], member.astype(BF), preferred_element_type=F32)
    block = (lax.broadcasted_iota(jnp.int32, (ROWS, 128), 0) // TB).astype(F32)
    place = jnp.where(member > 0.5, block * CAP + rank, -1000.0)
    slot = lax.broadcasted_iota(jnp.int32, (ROWS, SLOTS), 1).astype(F32)
    pick = (slot == place[:, 0:1]) | (slot == place[:, 1:2] + 80.0)
    pick = jnp.where(pick, 1.0, 0.0).astype(BF)
    st_ref[0] = pick
    w_ref[0] = weight
    half = SLOTS // 2
    for k, (part, width) in enumerate(((xa, W), (xb, W), (xc[:, : D - 2 * W], D - 2 * W))):
        got = lax.dot_general(pick, part, (((0,), (0,)), ((), ())), preferred_element_type=F32)
        got = got.astype(BF)
        rows_ref[0, 0, :, k * W : k * W + width] = got[:half]
        rows_ref[1, 0, :, k * W : k * W + width] = got[half:]


def select_rows(first, x0, x1, x2):
    rows = jnp.arange(ROWS, dtype=jnp.int32)
    tri = (rows[:, None] > rows[None, :]) & (rows[:, None] // TB == rows[None, :] // TB)
    return pl.pallas_call(
        select_kernel,
        grid=(2, 4, 2),
        out_shape=(
            jax.ShapeDtypeStruct((2, GROUPS, SLOTS // 2, D), BF),
            jax.ShapeDtypeStruct((GROUPS, ROWS, SLOTS), BF),
            jax.ShapeDtypeStruct((GROUPS, ROWS, 128), F32),
        ),
        in_specs=[
            pl.BlockSpec(memory_space=pltpu.SMEM),
            pl.BlockSpec((1, 1, 2, 4, TB, W), lambda c, z, y: (c, z, y, 0, 0, 0)),
            pl.BlockSpec((1, 4, 1, 2, TB, W), lambda c, z, y: (c, 0, z, y, 0, 0)),
            pl.BlockSpec((1, 2, 4, 1, TB, W), lambda c, z, y: (c, y, 0, z, 0, 0)),
            pl.BlockSpec((ROWS, ROWS), lambda c, z, y: (0, 0)),
        ],
        out_specs=(
            pl.BlockSpec((2, 1, SLOTS // 2, D), lambda c, z, y: (0, c * 8 + z * 2 + y, 0, 0)),
            pl.BlockSpec((1, ROWS, SLOTS), lambda c, z, y: (c * 8 + z * 2 + y, 0, 0)),
            pl.BlockSpec((1, ROWS, 128), lambda c, z, y: (c * 8 + z * 2 + y, 0, 0)),
        ),
        compiler_params=pltpu.CompilerParams(vmem_limit_bytes=56 << 20),
        name="select_rows",
    )(first, x0, x1, x2, tri.astype(BF))


def expand_kernel(st_ref, w_ref, h_ref, o_ref):
    pick = st_ref[0]
    zero = jnp.zeros((SLOTS // 2, HID), BF)
    both = jnp.concatenate(
        [
            jnp.concatenate([h_ref[0, 0], zero], axis=1),
            jnp.concatenate([zero, h_ref[1, 0]], axis=1),
        ],
        axis=0,
    )
    wide = jnp.dot(pick, both, preferred_element_type=F32)
    w = w_ref[0]
    left = (wide[:, :HID] * w[:, 0:1]).astype(BF)
    right = (wide[:, HID:] * w[:, 1:2]).astype(BF)
    o_ref[..., :HID] = left.reshape(1, 1, 2, 4, TB, HID)
    o_ref[..., HID:] = right.reshape(1, 1, 2, 4, TB, HID)


def expand_hidden(st, w, hidden):
    return pl.pallas_call(
        expand_kernel,
        grid=(2, 4, 2),
        out_shape=jax.ShapeDtypeStruct((2, 4, 4, 4, TB, 2 * HID), BF),
        in_specs=[
            pl.BlockSpec((1, ROWS, SLOTS), lambda c, z, y: (c * 8 + z * 2 + y, 0, 0)),
            pl.BlockSpec((1, ROWS, 128), lambda c, z, y: (c * 8 + z * 2 + y, 0, 0)),
            pl.BlockSpec((2, 1, SLOTS // 2, HID), lambda c, z, y: (0, c * 8 + z * 2 + y, 0, 0)),
        ],
        out_specs=pl.BlockSpec((1, 1, 2, 4, TB, 2 * HID), lambda c, z, y: (c, z, y, 0, 0, 0)),
        name="expand_hidden",
    )(st, w, hidden)


KINDS = (
    (2, 2), (2, 1), (2, 3), (1, 2), (3, 2), (2, 0), (1, 1), (3, 1),
    (1, 3), (3, 3), (0, 2), (1, 0), (3, 0), (0, 1), (0, 3), (0, 0),
)
STEPS = 3 * len(KINDS)
NS = 9
NR = 4


def scatter_kernel(
    hw, wd, out, acc, hown, hsib, ssend, srecv, slots, ab, cbuf, dbuf, ebuf, fbuf, gbuf, tbuf,
    hbuf, ibuf, jbuf, hsem, s_send, s_recv, credit, slot_sem, ab_sem, c_sem, d_sem, e_sem,
    f_sem, g_sem, t_send, t_recv,
):
    step, sibling = places()

    def pick(values, index):
        total = jnp.int32(values[0])
        for i in range(1, len(values)):
            total = jnp.where(index == i, jnp.int32(values[i]), total)
        return total

    dev = {}
    for pos in range(3):
        for by in (1, -1):
            dev[pos, by] = [step(ORDER[k][pos], by) for k in range(3)]

    def device(pos, by, k):
        options = dev[pos, by]
        return tuple(
            jnp.where(k == 0, options[0][i], jnp.where(k == 1, options[1][i], options[2][i]))
            for i in range(3)
        )

    def third_second(i):
        kind = i // 3
        return pick([v[0] for v in KINDS], kind), pick([v[1] for v in KINDS], kind)

    def fetch(i, core, buf, sem):
        k = lax.rem(i, 3)
        dc, db = third_second(i)
        at = lax.rem(i, 2)

        @pl.when(k == 0)
        def _():
            pltpu.make_async_copy(hw.at[core, dc, db], buf.at[at], sem.at[at]).start()

        @pl.when(k == 1)
        def _():
            pltpu.make_async_copy(hw.at[core, db, :, dc], buf.at[at], sem.at[at]).start()

        @pl.when(k == 2)
        def _():
            pltpu.make_async_copy(hw.at[core, :, dc, db], buf.at[at], sem.at[at]).start()

    def fetched(i, buf, sem):
        at = lax.rem(i, 2)
        pltpu.make_async_copy(hw.at[0, 0, 0], buf.at[at], sem.at[at]).wait()

    def product(h, k, put):
        def block(n, _):
            col = pl.multiple_of(k * W + n * 128, 128)
            total = lax.dot_general(
                h[:, :HID], wd[0, pl.ds(col, 256)], (((1,), (1,)), ((), ())),
                preferred_element_type=F32,
            )
            total = total + lax.dot_general(
                h[:, HID:], wd[1, pl.ds(col, 256)], (((1,), (1,)), ((), ())),
                preferred_element_type=F32,
            )
            put(pl.multiple_of(n * 128, 128), total)
            return 0

        def outer(j, _):
            return block(jnp.minimum(2 * j, jnp.where(k == 2, 8, W // 128 - 2)), 0)

        lax.fori_loop(0, 6, outer, 0)

    def sib_copy(i):
        return pltpu.make_async_remote_copy(
            src_ref=ssend.at[lax.rem(i, 2)],
            dst_ref=srecv.at[lax.rem(i, NR)],
            send_sem=s_send.at[lax.rem(i, 2)],
            recv_sem=s_recv.at[lax.rem(i, NR)],
            device_id=sibling,
            device_id_type=MESH,
        )

    def sib_part(i):
        fetched(i, hsib, hsem.at[1])

        @pl.when(i + 1 < STEPS)
        def _():
            fetch(i + 1, 1, hsib, hsem.at[1])

        @pl.when(i >= 2)
        def _():
            sib_copy(i).wait_send()

        k = lax.rem(i, 3)
        at = lax.rem(i, 2)

        def put(col, total):
            ssend[at, :, :, pl.ds(col, 256)] = total.astype(BF).reshape(4, TB, 256)

        product(hsib[at].reshape(4 * TB, 2 * HID), k, put)

        @pl.when(i >= NR)
        def _():
            pl.semaphore_wait(credit, 1)

        sib_copy(i).start()

    def half(src, dst, which, send, recv, to):
        return pltpu.make_async_remote_copy(
            src_ref=src.at[pl.ds(2 * which, 2)],
            dst_ref=dst.at[pl.ds(2 * which, 2)],
            send_sem=send.at[which],
            recv_sem=recv.at[which],
            device_id=to,
            device_id_type=MESH,
        )

    def arrived(dst, sem, which):
        half(dst, dst, which, sem, sem, sibling).wait_recv()

    def total_rows(i, which, refs, put):
        def body(r, _):
            v = acc[r] + srecv[lax.rem(i, NR), r].astype(F32)
            for ref in refs:
                v = v + ref[r].astype(F32)
            put(r, v.astype(BF))
            return 0

        lax.fori_loop(2 * which, 2 * which + 2, body, 0)

    def own_part(i):
        k = lax.rem(i, 3)
        dc, db = third_second(i)
        at = lax.rem(i, 2)
        slot = lax.rem(i, NS)
        fetched(i, hown, hsem.at[0])

        @pl.when(i + 1 < STEPS)
        def _():
            fetch(i + 1, 0, hown, hsem.at[0])

        def put_acc(col, total):
            acc[:, :, pl.ds(col, 256)] = total.reshape(4, TB, 256)

        product(hown[at].reshape(4 * TB, 2 * HID), k, put_acc)
        sib_copy(i).wait_recv()
        buf = slots.at[slot]

        @pl.when((i >= NS) & (i < STEPS - 3))
        def _():
            for which in range(2):
                half(buf, buf, which, slot_sem.at[slot], slot_sem.at[slot], sibling).wait_send()

        def put(r, v):
            buf[r] = v

        def send(dst, recv, tos):
            for which in range(2):
                half(buf, dst, which, slot_sem.at[slot], recv, tos[which]).start()

        down = lambda pos: device(pos, -1, k)
        up = lambda pos: device(pos, 1, k)

        @pl.when(dc == 2)
        def _():
            total_rows(i, 0, [], put)
            total_rows(i, 1, [], put)
            send(ab.at[k, db], ab_sem.at[k, db], (down(2), up(2)))

        @pl.when(dc == 1)
        def _():
            arrived(ab.at[k, db], ab_sem.at[k, db], 0)
            total_rows(i, 0, [ab.at[k, db]], put)
            total_rows(i, 1, [], put)
            send(cbuf.at[k, db], c_sem.at[k, db], (down(2), down(2)))

        @pl.when(dc == 3)
        def _():
            arrived(ab.at[k, db], ab_sem.at[k, db], 1)
            total_rows(i, 0, [], put)
            total_rows(i, 1, [ab.at[k, db]], put)
            send(dbuf.at[k, db], d_sem.at[k, db], (up(2), up(2)))

        @pl.when(dc == 0)
        def _():
            for which in range(2):
                arrived(cbuf.at[k, db], c_sem.at[k, db], which)
                arrived(dbuf.at[k, db], d_sem.at[k, db], which)

        cd = [cbuf.at[k, db], dbuf.at[k, db]]

        @pl.when((dc == 0) & (db == 2))
        def _():
            total_rows(i, 0, cd, put)
            total_rows(i, 1, cd, put)
            send(ebuf.at[k], e_sem.at[k], (down(1), up(1)))

        @pl.when((dc == 0) & (db == 1))
        def _():
            arrived(ebuf.at[k], e_sem.at[k], 0)
            total_rows(i, 0, cd + [ebuf.at[k]], put)
            total_rows(i, 1, cd, put)
            send(fbuf.at[k], f_sem.at[k], (down(1), down(1)))

        @pl.when((dc == 0) & (db == 3))
        def _():
            arrived(ebuf.at[k], e_sem.at[k], 1)
            total_rows(i, 0, cd, put)
            total_rows(i, 1, cd + [ebuf.at[k]], put)
            send(gbuf.at[k], g_sem.at[k], (up(1), up(1)))

        @pl.when((dc == 0) & (db == 0))
        def _():
            for which in range(2):
                arrived(fbuf.at[k], f_sem.at[k], which)
                arrived(gbuf.at[k], g_sem.at[k], which)

            def put_t(r, v):
                tbuf[k, r] = v

            for which in range(2):
                total_rows(i, which, cd + [fbuf.at[k], gbuf.at[k]], put_t)

        @pl.when(i + NR < STEPS)
        def _():
            pl.semaphore_signal(credit, inc=1, device_id=sibling, device_id_type=MESH)

    fetch(jnp.int32(0), 1, hsib, hsem.at[1])
    fetch(jnp.int32(0), 0, hown, hsem.at[0])
    greet(step, sibling)
    sib_part(jnp.int32(0))

    def body(i, _):
        @pl.when(i + 1 < STEPS)
        def _():
            sib_part(i + 1)

        own_part(i)
        return 0

    lax.fori_loop(0, STEPS, body, 0)

    def tail(k, idx, src, dst, to):
        return pltpu.make_async_remote_copy(
            src_ref=src,
            dst_ref=dst,
            send_sem=t_send.at[k, idx],
            recv_sem=t_recv.at[k, idx],
            device_id=to,
            device_id_type=MESH,
        )

    lo, hi = pl.ds(0, H2), pl.ds(H2, H2)
    tails = []
    for k in range(3):
        down, up = step(ORDER[k][0], -1), step(ORDER[k][0], 1)
        tails.append(
            (
                tail(k, 0, tbuf.at[k, 2, lo], hbuf.at[k, lo], down),
                tail(k, 1, tbuf.at[k, 2, hi], hbuf.at[k, hi], up),
                tail(k, 2, tbuf.at[k, 1], ibuf.at[k], down),
                tail(k, 3, tbuf.at[k, 3], jbuf.at[k], up),
            )
        )
        tails[k][0].start()
        tails[k][1].start()
    for k in range(3):
        tails[k][0].wait_recv()
        tbuf[k, 1, lo] = (tbuf[k, 1, lo].astype(F32) + hbuf[k, lo].astype(F32)).astype(BF)
        tails[k][2].start()
        tails[k][1].wait_recv()
        tbuf[k, 3, hi] = (tbuf[k, 3, hi].astype(F32) + hbuf[k, hi].astype(F32)).astype(BF)
        tails[k][3].start()
    for k in range(3):
        tails[k][2].wait_recv()
        tails[k][3].wait_recv()
        width = min(W, D - k * W)
        v = tbuf[k, 0].astype(F32) + ibuf[k].astype(F32) + jbuf[k].astype(F32)
        out[:, k * W : k * W + width] = v.astype(BF)[:, :width]
    for k in range(3):
        for cp in tails[k]:
            cp.wait_send()
    for at in range(2):
        sib_copy(jnp.int32(at)).wait_send()
    for at in range(NS):
        for which in range(2):
            buf = slots.at[at]
            half(buf, buf, which, slot_sem.at[at], slot_sem.at[at], sibling).wait_send()


def scatter_sums(hw, wd):
    piece = (4, TB, W)
    dma = pltpu.SemaphoreType.DMA
    return pl.pallas_call(
        scatter_kernel,
        out_shape=jax.ShapeDtypeStruct((TB, D), BF),
        in_specs=[pl.BlockSpec(memory_space=pl.ANY), pl.BlockSpec(memory_space=pltpu.VMEM)],
        out_specs=pl.BlockSpec(memory_space=pltpu.VMEM),
        scratch_shapes=[
            pltpu.VMEM(piece, F32),
            pltpu.VMEM((2, 4, TB, 2 * HID), BF),
            pltpu.VMEM((2, 4, TB, 2 * HID), BF),
            pltpu.VMEM((2,) + piece, BF),
            pltpu.VMEM((NR,) + piece, BF),
            pltpu.VMEM((NS,) + piece, BF),
            pltpu.VMEM((3, 4) + piece, BF),
            pltpu.VMEM((3, 4) + piece, BF),
            pltpu.VMEM((3, 4) + piece, BF),
            pltpu.VMEM((3,) + piece, BF),
            pltpu.VMEM((3,) + piece, BF),
            pltpu.VMEM((3,) + piece, BF),
            pltpu.VMEM((3,) + piece, BF),
            pltpu.VMEM((3, TB, W), BF),
            pltpu.VMEM((3, TB, W), BF),
            pltpu.VMEM((3, TB, W), BF),
            dma((2, 2)),
            dma((2,)),
            dma((NR,)),
            pltpu.SemaphoreType.REGULAR,
            dma((NS, 2)),
            dma((3, 4, 2)),
            dma((3, 4, 2)),
            dma((3, 4, 2)),
            dma((3, 2)),
            dma((3, 2)),
            dma((3, 2)),
            dma((3, 4)),
            dma((3, 4)),
        ],
        compiler_params=pltpu.CompilerParams(
            collective_id=2, has_side_effects=True, vmem_limit_bytes=67043328
        ),
        name="scatter_sums",
    )(hw, wd)


def per_device(prm_tokens, expert_ids, combine_weights, w_gate, w_up, w_down):
    cut = functools.partial(lax.reduce_precision, exponent_bits=8, mantissa_bits=7)
    high = cut(combine_weights)
    mid = cut(combine_weights - high)
    low = combine_weights - high - mid
    meta = jnp.concatenate([expert_ids.astype(F32), high, mid, low], axis=1).astype(BF)
    meta = jnp.pad(meta, ((0, 0), (0, 128 - 32)))
    xs = jnp.concatenate([prm_tokens, meta], axis=1).reshape(TB, 3, W).transpose(1, 0, 2)
    x0, x1, x2 = gather_tokens(xs)
    first = 2 * (lax.axis_index("tp") * 4 + lax.axis_index("ep"))
    rows, st, w = select_rows(first.astype(jnp.int32)[None], x0, x1, x2)
    flat = rows.reshape(2, GROUPS * SLOTS // 2, D)
    gate = jnp.einsum("jcd,jdh->jch", flat, w_gate, preferred_element_type=F32)
    up = jnp.einsum("jcd,jdh->jch", flat, w_up, preferred_element_type=F32)
    hidden = (jax.nn.silu(gate) * up).astype(BF).reshape(2, GROUPS, SLOTS // 2, HID)
    hw = expand_hidden(st, w, hidden)
    return scatter_sums(hw, w_down)


def solution(mesh):
    in_specs = (
        P(("rep", "tp", "ep"), None),
        P(("rep", "tp", "ep"), None),
        P(("rep", "tp", "ep"), None),
        P(("tp", "ep"), None, "rep"),
        P(("tp", "ep"), None, "rep"),
        P(("tp", "ep"), None, "rep"),
    )
    out_specs = P(("rep", "tp", "ep"), None)
    return jax.shard_map(
        per_device, mesh=mesh, in_specs=in_specs, out_specs=out_specs, check_vma=False
    )
```
